32 devices in a mesh: design: 2 (over x), gx: 4 (over y, core), gy: 4 (over z).
Axes of the slice: x: 2, y: 2, z: 4, core: 2. Of those that a mesh axis runs over, the one named last changes fastest.
Arguments:
- e_field: float32 [6, 16, 64, 512], P('design', None, 'gx', 'gy'), parts along dimension 0, may hold values from -6 to 6
- h_field: float32 [6, 16, 64, 512], P('design', None, 'gx', 'gy'), parts along dimension 0, may hold values from -6 to 6
- inverse_permittivity: float32 [32, 64, 512], P('design', 'gx', 'gy'), parts along dimension 0, may hold values from 0.0833 to 1
- monitor_layer: int32 [128, 512], P(('design', 'gx'), 'gy'), parts along dimension 0, may hold values from 0 to 15
- source_layer: int32 [128, 512], P(('design', 'gx'), 'gy'), parts along dimension 0, may hold values from 0 to 15
- residual_far: float32 [4, 2, 2, 256, 256], P('design', None, None, 'gx', 'gy'), parts along dimension 0, may hold values from -6 to 6
Outputs:
- e_forward: float32 [6, 16, 64, 512], P('design', None, 'gx', 'gy'), parts along dimension 0
- far_field: float32 [4, 2, 2, 256, 256], P('design', None, None, 'gx', 'gy'), parts along dimension 0
- e_adjoint: float32 [6, 16, 64, 512], P('design', None, 'gx', 'gy'), parts along dimension 0
The draws below stay inside these ranges and needn't reach their ends.
There are 2 independent parts, one for each index of `design`. The reference program is written for one: setup_inputs(seed, part) draws one part's arguments, and reference() takes and returns one part's arrays. A program takes and returns all parts, laid end to end along the dimension named above; each array names one. Nothing has to cross between parts.
All inputs are finite; a program needn't handle non-finite values.
Results may differ from the reference program's by a relative error of at most 0.0001.
Values sent between devices are 32-bit elements; how exact they have to be, the bound alone decides.
No kernel may reach another device: no remote copies, remote signals or barrier semaphores. Data moves between devices by JAX's collectives and lax.ppermute only.
A program may use at most 64 MiB of HBM per device.

```python
import math
import jax
import jax.numpy as jnp
from jax import lax

NZ = 16
DIRS = 256
NX = 64
NY = 512


def set_ends(drawn, own_key, smallest, largest):
    extent = drawn.shape
    spot = [jax.random.randint(jax.random.fold_in(own_key, axis), (), 0, extent[axis]) for axis in range(len(extent))]
    drawn = drawn.at[tuple(spot)].set(smallest)
    longest = extent.index(max(extent))
    spot[longest] = (spot[longest] + 1) % extent[longest]
    return drawn.at[tuple(spot)].set(largest)


def block_levels(key, dims, shards, smallest, largest):
    loudness, own = 1.0, jax.random.fold_in(key, 6)
    for dim, parts in shards:
        steps = jnp.exp(jax.random.uniform(jax.random.fold_in(own, dim), (parts,), jnp.float32, smallest / len(shards), largest / len(shards)))
        loudness = loudness * jnp.repeat(steps, dims[dim] // parts).reshape([-1 if axis == dim else 1 for axis in range(len(dims))])
    return loudness


def centred(key, dims, width, limit, split=(), kind=jnp.bfloat16):
    gain = block_levels(key, dims, split, -0.22, 0.18) if split else 1.0
    result = jax.random.normal(key, dims, jnp.float32) * width * gain
    return jnp.minimum(jnp.maximum(result, -limit), limit).astype(kind)


def setup_inputs(seed: int = 0, part: int = 0) -> dict:
    keys = jax.random.split(jax.random.key(seed), 7)
    part_keys = jax.random.split(jax.random.fold_in(keys[6], part), 7)
    e_field = centred(part_keys[0], (3, NZ, NX, NY), 1.0, 6.0, ((2, 4), (3, 4)), jnp.float32)
    h_field = centred(part_keys[1], (3, NZ, NX, NY), 1.0, 6.0, ((2, 4), (3, 4)), jnp.float32)
    inverse_permittivity = jnp.clip(jnp.exp(math.log(1.0) - 2.4853067 * jax.random.uniform(part_keys[2], (NZ, NX, NY), jnp.float32) ** block_levels(part_keys[2], (NZ, NX, NY), ((1, 4), (2, 4)), -0.2, 0.2)), 0.0833, 1.0)
    monitor_layer = set_ends(jax.random.randint(part_keys[3], (NX, NY), 0, NZ), jax.random.fold_in(part_keys[3], 1), 0, NZ - 1).astype(jnp.int32)
    source_layer = set_ends(jax.random.randint(part_keys[4], (NX, NY), 0, NZ), jax.random.fold_in(part_keys[4], 1), 0, NZ - 1).astype(jnp.int32)
    residual_far = centred(part_keys[5], (2, 2, 2, DIRS, DIRS), 1.0, 6.0, ((3, 4), (4, 4)), jnp.float32)
    return dict(e_field=e_field, h_field=h_field, inverse_permittivity=inverse_permittivity, monitor_layer=monitor_layer, source_layer=source_layer, residual_far=residual_far)


courant = 0.5
omegas = (0.7, 1.3)
factors = (3, 5)
highest = lax.Precision.HIGHEST

def contract(form, left, right):
    return jnp.einsum(form, left, right, precision=highest)

def ahead(field, along):
    count = field.shape[along]
    widths = [(0, 0)] * field.ndim
    widths[along] = (0, 1)
    return jnp.pad(lax.slice_in_dim(field, 1, count, axis=along), widths)

def behind(field, along):
    count = field.shape[along]
    widths = [(0, 0)] * field.ndim
    widths[along] = (1, 0)
    return jnp.pad(lax.slice_in_dim(field, 0, count - 1, axis=along), widths)

def phase_pair(rows, cols, length):
    cosines = []
    sines = []
    for factor in factors:
        index = jnp.mod((rows[:, None] - DIRS // 2) * cols[None, :] * factor, 4 * length)
        angle = index.astype(jnp.float32) * (2.0 * math.pi / (4 * length))
        cosines.append(jnp.cos(angle))
        sines.append(jnp.sin(angle))
    return (jnp.stack(cosines), jnp.stack(sines))

def step_magnetic(elec, magn):
    curl_x = ahead(elec[2], 2) - elec[2] - (ahead(elec[1], 0) - elec[1])
    curl_y = ahead(elec[0], 0) - elec[0] - (ahead(elec[2], 1) - elec[2])
    curl_z = ahead(elec[1], 1) - elec[1] - (ahead(elec[0], 2) - elec[0])
    return magn - courant * jnp.stack([curl_x, curl_y, curl_z])

def step_electric(elec, magn, inverse, current):
    curl_x = magn[2] - behind(magn[2], 2) - (magn[1] - behind(magn[1], 0))
    curl_y = magn[0] - behind(magn[0], 0) - (magn[2] - behind(magn[2], 1))
    curl_z = magn[1] - behind(magn[1], 1) - (magn[0] - behind(magn[0], 2))
    if current is not None:
        curl_x = curl_x - current[0]
        curl_y = curl_y - current[1]
    return elec + courant * inverse[None] * jnp.stack([curl_x, curl_y, curl_z])

def reference(e_field, h_field, inverse_permittivity, monitor_layer, source_layer, residual_far):
    elec = e_field
    magn = h_field
    watch = (jnp.arange(NZ, dtype=jnp.int32)[:, None, None] == monitor_layer[None]).astype(jnp.float32)
    planes = []
    for moment in range(2):
        magn = step_magnetic(elec, magn)
        elec = step_electric(elec, magn, inverse_permittivity, None)
        planes.append(lax.optimization_barrier(jnp.sum(elec[:2] * watch[None], axis=1)))
    e_forward = elec
    spec_real = jnp.stack([math.cos(omega) * planes[0] + math.cos(2 * omega) * planes[1] for omega in omegas])
    spec_imag = jnp.stack([-(math.sin(omega) * planes[0] + math.sin(2 * omega) * planes[1]) for omega in omegas])
    directions = jnp.arange(DIRS, dtype=jnp.int32)
    cos_x, sin_x = phase_pair(directions, jnp.arange(NX, dtype=jnp.int32), NX)
    cos_y, sin_y = phase_pair(directions, jnp.arange(NY, dtype=jnp.int32), NY)
    q_real = contract('fax,fcxy->fcay', cos_x, spec_real) + contract('fax,fcxy->fcay', sin_x, spec_imag)
    q_imag = contract('fax,fcxy->fcay', cos_x, spec_imag) - contract('fax,fcxy->fcay', sin_x, spec_real)
    a_real = contract('fcay,fby->fcab', q_real, cos_y) + contract('fcay,fby->fcab', q_imag, sin_y)
    a_imag = contract('fcay,fby->fcab', q_imag, cos_y) - contract('fcay,fby->fcab', q_real, sin_y)
    far_field = jnp.stack([a_real, a_imag], axis=2) * (1.0 / math.sqrt(NX * NY))
    res_real = residual_far[:, :, 0]
    res_imag = residual_far[:, :, 1]
    u_real = contract('fcab,fby->fcay', res_real, cos_y) - contract('fcab,fby->fcay', res_imag, sin_y)
    u_imag = contract('fcab,fby->fcay', res_real, sin_y) + contract('fcab,fby->fcay', res_imag, cos_y)
    s_real = (contract('fax,fcay->fcxy', cos_x, u_real) - contract('fax,fcay->fcxy', sin_x, u_imag)) / DIRS
    s_imag = (contract('fax,fcay->fcxy', cos_x, u_imag) + contract('fax,fcay->fcxy', sin_x, u_real)) / DIRS
    layers = (jnp.arange(NZ, dtype=jnp.int32)[:, None, None] == source_layer[None]).astype(jnp.float32)
    elec = jnp.zeros_like(e_field)
    magn = jnp.zeros_like(h_field)
    for moment in range(2):
        tick = moment + 1
        drive = s_real[0] * math.cos(omegas[0] * tick) - s_imag[0] * math.sin(omegas[0] * tick)
        drive = drive + s_real[1] * math.cos(omegas[1] * tick) - s_imag[1] * math.sin(omegas[1] * tick)
        current = layers[None] * drive[:, None]
        magn = step_magnetic(elec, magn)
        elec = step_electric(elec, magn, inverse_permittivity, current)
    return (e_forward, far_field, elec)
```

```python
import functools
import math

import jax
import jax.numpy as jnp
from jax import lax
from jax.experimental import pallas as pl
from jax.experimental.pallas import tpu as pltpu
from jax.sharding import PartitionSpec as P

NZ = 16
DIRS = 256
HALF = 0.5
OMEGAS = (0.7, 1.3)
FACTORS = (3, 5)
HIGHEST = lax.Precision.HIGHEST
F32 = jnp.float32
LANES = 128
GROUP = 8


def iota(shape, dim):
    return lax.broadcasted_iota(jnp.int32, shape, dim)


def cos_turn(index, length):
    bits = length.bit_length() - 1
    quadrant = lax.shift_right_arithmetic(index + length // 2, bits)
    rest = index - lax.shift_left(quadrant, bits)
    angle = rest.astype(F32) * (0.5 * math.pi / length)
    sq = angle * angle
    cosine = 1.0 + sq * (-0.5 + sq * (1 / 24 + sq * (-1 / 720 + sq * (1 / 40320))))
    sine = angle * (1.0 + sq * (-1 / 6 + sq * (1 / 120 + sq * (-1 / 5040 + sq * (1 / 362880)))))
    value = jnp.where((quadrant & 1) == 1, sine, cosine)
    return jnp.where(((quadrant + 1) & 2) == 2, -value, value)


def dot(left, right):
    return jnp.dot(left, right, precision=HIGHEST, preferred_element_type=F32)


def swap(value, half):
    if 2 * half == LANES:
        return pltpu.roll(value, half, 1)
    return jnp.concatenate([value[:, half:], value[:, :half]], axis=1)


def call(kernel, name, out, scratch=()):
    single = isinstance(out[0], int)
    shapes = [jax.ShapeDtypeStruct(s, F32) for s in ([out] if single else out)]
    return pl.pallas_call(
        kernel,
        out_shape=shapes[0] if single else tuple(shapes),
        scratch_shapes=list(scratch),
        name=name,
    )


def pack_edges(e, h, k, layer, up, down, own, *, cx):
    def rows(ref, count, x, first=0):
        return ref[pl.ds(first * NZ * cx + x, count * NZ, stride=cx), :]

    up[0 : 3 * NZ] = rows(e, 3, cx - 1)
    up[3 * NZ : 6 * NZ] = rows(h, 3, cx - 1)
    up[6 * NZ : 7 * NZ] = rows(k, 1, cx - 1)
    up[7 * NZ : 10 * NZ] = rows(e, 3, cx - 2)
    up[10 * NZ : 12 * NZ] = rows(h, 2, cx - 2, 1)
    down[0 : 3 * NZ] = rows(e, 3, 0)
    down[3 * NZ : 6 * NZ] = rows(h, 3, 0)
    down[6 * NZ : 7 * NZ] = rows(k, 1, 0)
    down[7 * NZ : 9 * NZ] = rows(e, 2, 1, 1)
    lane = iota((cx, LANES), 1)
    width = e.shape[1]

    def shifted(plane, amount):
        return pltpu.roll(plane, amount % width, 1)[:, :LANES]

    for field in range(7):
        ref = (e, h, k)[field // 3]
        base = (field % 3) * NZ
        packed = jnp.zeros((cx, LANES), F32)
        for z in range(NZ):
            plane = ref[(base + z) * cx : (base + z + 1) * cx, :]
            hit = (lane >= GROUP * z) & (lane < GROUP * z + 4)
            packed = jnp.where(hit, shifted(plane, GROUP * z + 2), packed)
        own[field * cx : (field + 1) * cx] = packed
    layers = layer[...].astype(F32)
    packed = jnp.where(lane < 4, shifted(layers, 2), 0.0)
    for amount in (8, 16, 32, 64):
        packed = packed + pltpu.roll(packed, amount, 1)
    own[7 * cx : 8 * cx] = packed
    for field in range(8):
        up[12 * NZ + 2 * field : 12 * NZ + 2 * field + 2] = own[field * cx + cx - 2 : field * cx + cx]
        down[9 * NZ + 2 * field : 9 * NZ + 2 * field + 2] = own[field * cx : field * cx + 2]
    up[12 * NZ + 16 : 12 * NZ + 24] = jnp.broadcast_to(layers[cx - 1 : cx, :], (8, width))
    down[9 * NZ + 16 : 9 * NZ + 24] = jnp.broadcast_to(layers[0:1, :], (8, width))


def pack_strips(own, before, after, up, down, ext, *, cx):
    rows = cx + 8
    first = lax.axis_index("gx") == 0
    last = lax.axis_index("gx") == lax.axis_size("gx") - 1
    lane = iota((rows, LANES), 1) % GROUP
    packed = [[None, None], [None, None]]
    for field in range(8):
        base = field * rows
        ext[base : base + cx] = own[field * cx : (field + 1) * cx]
        ext[base + cx : base + rows] = jnp.zeros((8, LANES), F32)
        late = after[9 * NZ + 2 * field : 9 * NZ + 2 * field + 2]
        ext[base + cx : base + cx + 2] = jnp.where(last, 0.0, late)
        early = before[12 * NZ + 2 * field : 12 * NZ + 2 * field + 2]
        ext[base + rows - 2 : base + rows] = jnp.where(first, 0.0, early)
        strip = ext[base : base + rows]
        group, slot = divmod(field, 4)
        hit = lane // 2 == slot
        for side, amount in ((0, 2 * slot), (1, 2 * slot - 2)):
            moved = pltpu.roll(strip, amount % LANES, 1) if amount else strip
            old = packed[side][group]
            packed[side][group] = moved if old is None else jnp.where(hit, moved, old)
    for group in range(2):
        up[group * rows : (group + 1) * rows] = packed[0][group]
        down[group * rows : (group + 1) * rows] = packed[1][group]


def forward(
    e, h, k, layer, monitor, before, after, own, left, right,
    out, planes, kext, kstrip, lext, lstrip, fe, fh, *, cx
):
    rows = cx + 8
    gx, gy = lax.axis_index("gx"), lax.axis_index("gy")
    first_x, last_x = gx == 0, gx == lax.axis_size("gx") - 1
    first_y, last_y = gy == 0, gy == lax.axis_size("gy") - 1
    width = e.shape[1]
    for dst, src, count in ((fe, e, 3 * NZ), (fh, h, 3 * NZ), (kext, k, NZ)):
        for p in range(count):
            dst[p * rows : p * rows + cx] = src[p * cx : (p + 1) * cx]

    def put(dst, plane, count, row, value, outside):
        dst[pl.ds(plane * rows + row, count, stride=rows), :] = jnp.where(outside, 0.0, value)

    put(fe, 0, 3 * NZ, cx, after[0 : 3 * NZ], last_x)
    put(fh, 0, 3 * NZ, cx, after[3 * NZ : 6 * NZ], last_x)
    put(kext, 0, NZ, cx, after[6 * NZ : 7 * NZ], last_x)
    put(fe, NZ, 2 * NZ, cx + 1, after[7 * NZ : 9 * NZ], last_x)
    put(fe, 0, 3 * NZ, rows - 1, before[0 : 3 * NZ], first_x)
    put(fh, 0, 3 * NZ, rows - 1, before[3 * NZ : 6 * NZ], first_x)
    put(kext, 0, NZ, rows - 1, before[6 * NZ : 7 * NZ], first_x)
    put(fe, 0, 3 * NZ, rows - 2, before[7 * NZ : 10 * NZ], first_x)
    put(fh, NZ, 2 * NZ, rows - 2, before[10 * NZ : 12 * NZ], first_x)
    lext[0:cx] = layer[...].astype(F32)
    lext[cx:rows] = after[9 * NZ + 16 : 9 * NZ + 24]
    lext[rows - 1 : rows] = before[12 * NZ + 16 : 12 * NZ + 17]

    lane = iota((rows, LANES), 1)
    column = lane % GROUP
    strips = []
    for field in range(8):
        group, slot = divmod(field, 4)
        mine = own[field * rows : (field + 1) * rows]
        low = jnp.where(first_y, 0.0, left[group * rows : (group + 1) * rows])
        high = jnp.where(last_y, 0.0, right[group * rows : (group + 1) * rows])
        low = pltpu.roll(low, (-2 * slot) % LANES, 1) if slot else low
        high = pltpu.roll(high, (6 - 2 * slot) % LANES, 1) if slot != 3 else high
        value = jnp.where(column < 4, mine, pltpu.roll(mine, 4, 1))
        value = jnp.where(column < 2, low, jnp.where(column >= 6, high, value))
        strips.append(value)
    kstrip[...] = strips[6]
    lstrip[...] = strips[7]
    es, hs, ks = strips[0:3], strips[3:6], HALF * strips[6]

    row = iota((rows, width), 0)
    inside = jnp.logical_not(first_x & (row >= rows - 2))
    row = iota((rows, LANES), 0)
    inside_strip = jnp.logical_not((first_x & (row >= rows - 2)) | (first_y & (column < 2)))
    wide_lane = iota((rows, width), 1)
    shown = monitor[...]

    def next_x(v):
        return pltpu.roll(v, rows - 1, 0)

    def prev_x(v):
        return pltpu.roll(v, 1, 0)

    def strip_to(strip, source, target):
        moved = pltpu.roll(strip, (target - source) % LANES, 1)
        if width == LANES:
            return moved
        return jnp.concatenate([moved] * (width // LANES), axis=1)

    def next_y(v, strip, z):
        edge = strip_to(strip, GROUP * z + 6, (width - 1) % LANES)
        return jnp.where(wide_lane == width - 1, edge, pltpu.roll(v, width - 1, 1))

    def prev_y(v, strip, z):
        edge = strip_to(strip, GROUP * z + 1, 0)
        return jnp.where(wide_lane == 0, edge, pltpu.roll(v, 1, 1))

    def strip_next_y(v):
        return pltpu.roll(v, LANES - 1, 1)

    def strip_prev_y(v):
        return pltpu.roll(v, 1, 1)

    def strip_next_z(v):
        return jnp.where(lane >= LANES - GROUP, 0.0, pltpu.roll(v, LANES - GROUP, 1))

    def strip_prev_z(v):
        return jnp.where(lane < GROUP, 0.0, pltpu.roll(v, GROUP, 1))

    def load(ref, comp, z):
        p = comp * NZ + z
        return ref[p * rows : (p + 1) * rows]

    for moment in range(2):
        ex, ey, ez = es
        hx, hy, hz = hs
        hx = hx - HALF * ((strip_next_y(ez) - ez) - (strip_next_z(ey) - ey))
        hy = hy - HALF * ((strip_next_z(ex) - ex) - (next_x(ez) - ez))
        hz = hz - HALF * ((next_x(ey) - ey) - (strip_next_y(ex) - ex))
        new_h = [jnp.where(inside_strip, v, 0.0) for v in (hx, hy, hz)]
        hx, hy, hz = new_h
        new_e = [
            ex + ks * ((hz - strip_prev_y(hz)) - (hy - strip_prev_z(hy))),
            ey + ks * ((hx - strip_prev_z(hx)) - (hz - prev_x(hz))),
            ez + ks * ((hy - prev_x(hy)) - (hx - strip_prev_y(hx))),
        ]
        seen_x = jnp.zeros((cx, width), F32)
        seen_y = jnp.zeros((cx, width), F32)
        zero = jnp.zeros((rows, width), F32)
        under_x, under_y = zero, zero
        ex, ey, ez = (load(fe, c, 0) for c in range(3))
        for z in range(NZ):
            above = [load(fe, c, z + 1) for c in range(3)] if z + 1 < NZ else [zero] * 3
            hx, hy, hz = (load(fh, c, z) for c in range(3))
            hx = hx - HALF * ((next_y(ez, es[2], z) - ez) - (above[1] - ey))
            hy = hy - HALF * ((above[0] - ex) - (next_x(ez) - ez))
            hz = hz - HALF * ((next_x(ey) - ey) - (next_y(ex, es[0], z) - ex))
            hx, hy, hz = (jnp.where(inside, v, 0.0) for v in (hx, hy, hz))
            kz = HALF * kext[z * rows : (z + 1) * rows]
            ex = ex + kz * ((hz - prev_y(hz, new_h[2], z)) - (hy - under_y))
            ey = ey + kz * ((hx - under_x) - (hz - prev_x(hz)))
            ez = ez + kz * ((hy - prev_x(hy)) - (hx - prev_y(hx, new_h[0], z)))
            hit = shown == z
            seen_x = jnp.where(hit, ex[:cx], seen_x)
            seen_y = jnp.where(hit, ey[:cx], seen_y)
            for c, (ev, hv) in enumerate(((ex, hx), (ey, hy), (ez, hz))):
                p = c * NZ + z
                if moment == 0:
                    fe[p * rows : (p + 1) * rows] = ev
                    fh[p * rows : (p + 1) * rows] = hv
                else:
                    out[p * cx : (p + 1) * cx] = ev[:cx]
            under_x, under_y = hx, hy
            ex, ey, ez = above
        planes[2 * moment * cx : (2 * moment + 1) * cx] = seen_x
        planes[(2 * moment + 1) * cx : (2 * moment + 2) * cx] = seen_y
        es, hs = new_e, new_h


def tables(far_table, source_table, *, cy, dirs, count):
    gy = lax.axis_index("gy")
    length = cy * count
    wide = 2 * dirs
    for s in range(count):
        sender = (gy - s + count) % count
        for f, factor in enumerate(FACTORS):
            y = sender * cy + iota((cy, wide), 0)
            lane = iota((cy, wide), 1)
            b = gy * dirs + lane % dirs
            turn = (b - DIRS // 2) * factor * y - jnp.where(lane >= dirs, length, 0)
            far_table[s * cy : (s + 1) * cy, f * wide : (f + 1) * wide] = cos_turn(turn, length)
            line = iota((wide, cy + LANES), 0)
            lane = iota((wide, cy + LANES), 1)
            near = lane % GROUP
            near = jnp.where(near < 4, near - 2, near + cy - 6)
            y = gy * cy + jnp.where(lane < cy, lane, near)
            b = sender * dirs + line % dirs
            turn = (b - DIRS // 2) * factor * y + jnp.where(line >= dirs, length, 0)
            base = (s * 2 + f) * wide
            source_table[base : base + wide] = cos_turn(turn, length) * (1.0 / DIRS)


def project_y(*refs, cx, cy, dirs, count):
    blocks, table, out = refs[:count], refs[count], refs[count + 1]
    total = None
    for s in range(count):
        part = dot(blocks[s][...], table[s * cy : (s + 1) * cy])
        total = part if total is None else total + part
    wide = 2 * dirs
    sign = jnp.where(iota((2 * cx, wide), 1) < dirs, 1.0, -1.0)
    for f, omega in enumerate(OMEGAS):
        value = None
        for moment in range(2):
            tick = omega * (moment + 1)
            part = total[2 * cx * moment : 2 * cx * (moment + 1), f * wide : (f + 1) * wide]
            part = math.cos(tick) * (part * sign) - math.sin(tick) * swap(part, dirs)
            value = part if value is None else value + part
        out[f * 2 * cx : (f + 1) * 2 * cx] = value


def project_x(*refs, cx, dirs_x, dirs_y, count, scale):
    blocks, out = refs[:count], refs[count]
    gx = lax.axis_index("gx")
    length = cx * count
    wide = 2 * dirs_y
    lane = iota((dirs_x, 2 * length), 1)
    a = gx * dirs_x + iota((dirs_x, 2 * length), 0)
    slot = lane % length
    x = (gx - slot // cx + count) % count * cx + slot % cx
    sign = jnp.where(iota((length, wide), 1) < dirs_y, 1.0, -1.0)
    for f, factor in enumerate(FACTORS):
        turn = (a - DIRS // 2) * factor * x - jnp.where(lane >= length, length, 0)
        table = cos_turn(turn, length) * scale
        for c in range(2):
            base = (2 * f + c) * cx
            value = jnp.concatenate([ref[base : base + cx] for ref in blocks], axis=0)
            value = jnp.concatenate([value, swap(value, dirs_y) * sign], axis=0)
            field = dot(table, value)
            out[f, c, 0] = field[:, :dirs_y]
            out[f, c, 1] = field[:, dirs_y:]


def spread_x(residual, *outs, cx, dirs_x, dirs_y, count):
    gx = lax.axis_index("gx")
    length = cx * count
    rows = cx + 8
    lane = iota((count * rows, 2 * dirs_x), 1)
    line = iota((count * rows, 2 * dirs_x), 0)
    slot = line % rows
    slot = jnp.where(slot >= cx + 4, slot - rows, slot)
    x = (gx + line // rows) % count * cx + slot
    a = gx * dirs_x + lane % dirs_x
    for f, factor in enumerate(FACTORS):
        turn = (a - DIRS // 2) * factor * x - jnp.where(lane >= dirs_x, length, 0)
        table = cos_turn(turn, length)
        for c in range(2):
            real, imag = residual[f, c, 0], residual[f, c, 1]
            value = jnp.concatenate(
                [jnp.concatenate([real, imag], axis=1), jnp.concatenate([-imag, real], axis=1)], axis=0
            )
            part = dot(table, value)
            pair = 2 * f + c
            for s in range(count):
                base = s * rows
                outs[s][pair * cx : (pair + 1) * cx] = part[base : base + cx]
                edge = 4 * cx + 2 * pair
                outs[s][edge : edge + 1] = part[base + cx : base + cx + 1]
                outs[s][edge + 1 : edge + 2] = part[base + rows - 1 : base + rows]


def adjoint(*refs, cx, cy, dirs, count):
    blocks = refs[:count]
    table, kext, kstrip, lext, lstrip, out = refs[count : count + 6]
    rows = cx + 8
    wide = 2 * dirs
    first_x, first_y = lax.axis_index("gx") == 0, lax.axis_index("gy") == 0
    sign = jnp.where(iota((rows, wide), 1) < dirs, -1.0, 1.0)
    drive = None
    for s in range(count):
        for f, omega in enumerate(OMEGAS):
            parts = [[], []]
            for c in range(2):
                pair = 2 * f + c
                edge = 4 * cx + 2 * pair
                value = jnp.concatenate(
                    [
                        blocks[s][pair * cx : (pair + 1) * cx],
                        blocks[s][edge : edge + 1],
                        jnp.zeros((6, wide), F32),
                        blocks[s][edge + 1 : edge + 2],
                    ],
                    axis=0,
                )
                turned = swap(value, dirs) * sign
                for moment in range(2):
                    tick = omega * (moment + 1)
                    parts[moment].append(math.cos(tick) * value + math.sin(tick) * turned)
            left = jnp.concatenate(parts[0] + parts[1], axis=0)
            base = (s * 2 + f) * wide
            part = dot(left, table[base : base + wide])
            drive = part if drive is None else drive + part
    first = [-HALF * drive[c * rows : (c + 1) * rows] for c in range(2)]
    second = [drive[(2 + c) * rows : (2 + c) * rows + cx, :cy] for c in range(2)]
    ax, ay = (v[:, :cy] for v in first)
    sx, sy = (v[:, cy:] for v in first)
    row = iota((rows, cy), 0)
    inside = jnp.logical_not(first_x & (row >= rows - 2))
    lane = iota((rows, LANES), 1)
    row = iota((rows, LANES), 0)
    inside_strip = jnp.logical_not((first_x & (row >= rows - 2)) | (first_y & (lane % GROUP < 2)))
    wide_lane = iota((rows, cy), 1)
    layer = lext[...]

    hit = lstrip[...] == (lane // GROUP).astype(F32)
    ks = kstrip[...]
    sx = jnp.where(hit, sx * ks, 0.0)
    sy = jnp.where(hit, sy * ks, 0.0)

    def next_z(v):
        return jnp.where(lane >= LANES - GROUP, 0.0, pltpu.roll(v, LANES - GROUP, 1))

    def next_x(v):
        return pltpu.roll(v, rows - 1, 0)

    def prev_x(v):
        return pltpu.roll(v, 1, 0)

    def strip_to(strip, source, target):
        moved = pltpu.roll(strip, (target - source) % LANES, 1)
        if cy == LANES:
            return moved
        return jnp.concatenate([moved] * (cy // LANES), axis=1)

    hsx = jnp.where(inside_strip, HALF * (next_z(sy) - sy), 0.0)
    hsz = -HALF * ((next_x(sy) - sy) - (pltpu.roll(sx, LANES - 1, 1) - sx))
    hsz = jnp.where(inside_strip, hsz, 0.0)
    zero = jnp.zeros((rows, cy), F32)
    under_x, under_y = zero, zero

    def source(z):
        kz = kext[z * rows : (z + 1) * rows]
        hit = layer == float(z)
        return jnp.where(hit, ax * kz, 0.0), jnp.where(hit, ay * kz, 0.0)

    def prev_y(v, strip, z):
        edge = strip_to(strip, GROUP * z + 1, 0)
        return jnp.where(wide_lane == 0, edge, pltpu.roll(v, 1, 1))

    ex, ey = source(0)
    for z in range(NZ):
        above_x, above_y = source(z + 1) if z + 1 < NZ else (zero, zero)
        hx = HALF * (above_y - ey)
        hy = -HALF * (above_x - ex)
        edge = strip_to(sx, GROUP * z + 6, (cy - 1) % LANES)
        right = jnp.where(wide_lane == cy - 1, edge, pltpu.roll(ex, cy - 1, 1))
        hz = -HALF * ((next_x(ey) - ey) - (right - ex))
        hx, hy, hz = (jnp.where(inside, v, 0.0) for v in (hx, hy, hz))
        kz = HALF * kext[z * rows : z * rows + cx]
        hit = layer[:cx] == float(z)
        jx = jnp.where(hit, second[0], 0.0)
        jy = jnp.where(hit, second[1], 0.0)
        curl_x = (hz - prev_y(hz, hsz, z)) - (hy - under_y)
        curl_y = (hx - under_x) - (hz - prev_x(hz))
        curl_z = (hy - prev_x(hy)) - (hx - prev_y(hx, hsx, z))
        out[z * cx : (z + 1) * cx] = ex[:cx] + kz * (curl_x[:cx] - jx)
        out[(NZ + z) * cx : (NZ + z + 1) * cx] = ey[:cx] + kz * (curl_y[:cx] - jy)
        out[(2 * NZ + z) * cx : (2 * NZ + z + 1) * cx] = kz * curl_z[:cx]
        under_x, under_y = hx, hy
        ex, ey = above_x, above_y


def shift(value, axis, steps):
    count = lax.axis_size(axis)
    return lax.ppermute(value, axis, [(i, (i + steps) % count) for i in range(count)])


def gather(value, axis):
    return [value] + [shift(value, axis, s) for s in range(1, lax.axis_size(axis))]


def per_device(e_field, h_field, inverse_permittivity, monitor_layer, source_layer, residual_far):
    cx, cy = e_field.shape[2:]
    rows = cx + 8
    nx, ny = lax.axis_size("gx"), lax.axis_size("gy")
    dirs_x, dirs_y = residual_far.shape[3:]
    part = functools.partial
    e = e_field.reshape(3 * NZ * cx, cy)
    h = h_field.reshape(3 * NZ * cx, cy)
    k = inverse_permittivity.reshape(NZ * cx, cy)

    up, down, own = call(
        part(pack_edges, cx=cx), "pack_edges",
        [(12 * NZ + 24, cy), (9 * NZ + 24, cy), (8 * cx, LANES)],
    )(e, h, k, source_layer)
    before = shift(up, "gx", 1)
    after = shift(down, "gx", -1)

    pieces = call(
        part(spread_x, cx=cx, dirs_x=dirs_x, dirs_y=dirs_y, count=nx), "spread_x",
        [(4 * cx + 8, 2 * dirs_y)] * nx,
    )(residual_far)
    far_table, source_table = call(
        part(tables, cy=cy, dirs=dirs_y, count=ny), "tables",
        [(ny * cy, 4 * dirs_y), (ny * 4 * dirs_y, cy + LANES)],
    )()

    up, down, ext = call(
        part(pack_strips, cx=cx), "pack_strips",
        [(2 * rows, LANES), (2 * rows, LANES), (8 * rows, LANES)],
    )(own, before, after)
    left = shift(up, "gy", 1)
    right = shift(down, "gy", -1)

    mixed = pieces[0]
    for s in range(1, nx):
        mixed = mixed + shift(pieces[s], "gx", s)

    e_forward, planes, kext, kstrip, lext, lstrip = call(
        part(forward, cx=cx), "forward",
        [(3 * NZ * cx, cy), (4 * cx, cy), (NZ * rows, cy), (rows, LANES), (rows, cy), (rows, LANES)],
        [pltpu.VMEM((3 * NZ * rows, cy), F32), pltpu.VMEM((3 * NZ * rows, cy), F32)],
    )(e, h, k, source_layer, monitor_layer, before, after, ext, left, right)

    spectrum = call(
        part(project_y, cx=cx, cy=cy, dirs=dirs_y, count=ny), "project_y", (4 * cx, 2 * dirs_y)
    )(*gather(planes, "gy"), far_table)
    scale = 1.0 / math.sqrt(cx * nx * cy * ny)
    far_field = call(
        part(project_x, cx=cx, dirs_x=dirs_x, dirs_y=dirs_y, count=nx, scale=scale), "project_x",
        residual_far.shape,
    )(*gather(spectrum, "gx"))

    e_adjoint = call(
        part(adjoint, cx=cx, cy=cy, dirs=dirs_y, count=ny), "adjoint", (3 * NZ * cx, cy)
    )(*gather(mixed, "gy"), source_table, kext, kstrip, lext, lstrip)
    return (e_forward.reshape(e_field.shape), far_field, e_adjoint.reshape(e_field.shape))


def solution(mesh):
    in_specs = (
        P("design", None, "gx", "gy"),
        P("design", None, "gx", "gy"),
        P("design", "gx", "gy"),
        P(("design", "gx"), "gy"),
        P(("design", "gx"), "gy"),
        P("design", None, None, "gx", "gy"),
    )
    out_specs = (
        P("design", None, "gx", "gy"),
        P("design", None, None, "gx", "gy"),
        P("design", None, "gx", "gy"),
    )
    return jax.shard_map(
        per_device, mesh=mesh, in_specs=in_specs, out_specs=out_specs, check_vma=False
    )
```

```python
import functools
import math

import jax
import jax.numpy as jnp
from jax import lax
from jax.experimental import pallas as pl
from jax.experimental.pallas import tpu as pltpu
from jax.sharding import PartitionSpec as P

NZ = 16
DIRS = 256
HALF = 0.5
OMEGAS = (0.7, 1.3)
FACTORS = (3, 5)
HIGHEST = lax.Precision.HIGHEST
F32 = jnp.float32
LANES = 128
GROUP = 8


def iota(shape, dim):
    return lax.broadcasted_iota(jnp.int32, shape, dim)


def cos_turn(index, length):
    bits = length.bit_length() - 1
    quadrant = lax.shift_right_arithmetic(index + length // 2, bits)
    rest = index - lax.shift_left(quadrant, bits)
    angle = rest.astype(F32) * (0.5 * math.pi / length)
    sq = angle * angle
    cosine = 1.0 + sq * (-0.5 + sq * (1 / 24 + sq * (-1 / 720 + sq * (1 / 40320))))
    sine = angle * (1.0 + sq * (-1 / 6 + sq * (1 / 120 + sq * (-1 / 5040 + sq * (1 / 362880)))))
    value = jnp.where((quadrant & 1) == 1, sine, cosine)
    return jnp.where(((quadrant + 1) & 2) == 2, -value, value)


def dot(left, right):
    return jnp.dot(left, right, precision=HIGHEST, preferred_element_type=F32)


def swap(value, half):
    if 2 * half == LANES:
        return pltpu.roll(value, half, 1)
    return jnp.concatenate([value[:, half:], value[:, :half]], axis=1)


def call(kernel, name, out, scratch=(), far=(), far_out=()):
    single = isinstance(out[0], int)
    near = pl.BlockSpec(memory_space=pltpu.VMEM)
    shapes = []
    for i, shape in enumerate([out] if single else out):
        shapes.append(jax.ShapeDtypeStruct(shape, F32) if i in far_out else pltpu.VMEM(shape, F32))

    def run(*args):
        args = [
            x if i in far else pltpu.with_memory_space_constraint(x, pltpu.VMEM)
            for i, x in enumerate(args)
        ]
        return pl.pallas_call(
            kernel,
            out_shape=shapes[0] if single else tuple(shapes),
            in_specs=[near] * len(args),
            out_specs=near if single else tuple([near] * len(shapes)),
            scratch_shapes=list(scratch),
            name=name,
        )(*args)

    return run


def pack_edges(e, h, k, layer, up, down, own, *, cx):
    def rows(ref, count, x, first=0):
        return ref[pl.ds(first * NZ * cx + x, count * NZ, stride=cx), :]

    up[0 : 3 * NZ] = rows(e, 3, cx - 1)
    up[3 * NZ : 6 * NZ] = rows(h, 3, cx - 1)
    up[6 * NZ : 7 * NZ] = rows(k, 1, cx - 1)
    up[7 * NZ : 10 * NZ] = rows(e, 3, cx - 2)
    up[10 * NZ : 12 * NZ] = rows(h, 2, cx - 2, 1)
    down[0 : 3 * NZ] = rows(e, 3, 0)
    down[3 * NZ : 6 * NZ] = rows(h, 3, 0)
    down[6 * NZ : 7 * NZ] = rows(k, 1, 0)
    down[7 * NZ : 9 * NZ] = rows(e, 2, 1, 1)
    lane = iota((cx, LANES), 1)
    width = e.shape[1]

    def shifted(plane, amount):
        return pltpu.roll(plane, amount % width, 1)[:, :LANES]

    for field in range(7):
        ref = (e, h, k)[field // 3]
        base = (field % 3) * NZ
        packed = jnp.zeros((cx, LANES), F32)
        for z in range(NZ):
            plane = ref[(base + z) * cx : (base + z + 1) * cx, :]
            hit = (lane >= GROUP * z) & (lane < GROUP * z + 4)
            packed = jnp.where(hit, shifted(plane, GROUP * z + 2), packed)
        own[field * cx : (field + 1) * cx] = packed
    layers = layer[...].astype(F32)
    packed = jnp.where(lane < 4, shifted(layers, 2), 0.0)
    for amount in (8, 16, 32, 64):
        packed = packed + pltpu.roll(packed, amount, 1)
    own[7 * cx : 8 * cx] = packed
    for field in range(8):
        up[12 * NZ + 2 * field : 12 * NZ + 2 * field + 2] = own[field * cx + cx - 2 : field * cx + cx]
        down[9 * NZ + 2 * field : 9 * NZ + 2 * field + 2] = own[field * cx : field * cx + 2]
    up[12 * NZ + 16 : 12 * NZ + 24] = jnp.broadcast_to(layers[cx - 1 : cx, :], (8, width))
    down[9 * NZ + 16 : 9 * NZ + 24] = jnp.broadcast_to(layers[0:1, :], (8, width))


def pack_strips(own, before, after, up, down, ext, *, cx):
    rows = cx + 8
    first = lax.axis_index("gx") == 0
    last = lax.axis_index("gx") == lax.axis_size("gx") - 1
    lane = iota((rows, LANES), 1) % GROUP
    packed = [[None, None], [None, None]]
    for field in range(8):
        base = field * rows
        ext[base : base + cx] = own[field * cx : (field + 1) * cx]
        ext[base + cx : base + rows] = jnp.zeros((8, LANES), F32)
        late = after[9 * NZ + 2 * field : 9 * NZ + 2 * field + 2]
        ext[base + cx : base + cx + 2] = jnp.where(last, 0.0, late)
        early = before[12 * NZ + 2 * field : 12 * NZ + 2 * field + 2]
        ext[base + rows - 2 : base + rows] = jnp.where(first, 0.0, early)
        strip = ext[base : base + rows]
        group, slot = divmod(field, 4)
        hit = lane // 2 == slot
        for side, amount in ((0, 2 * slot), (1, 2 * slot - 2)):
            moved = pltpu.roll(strip, amount % LANES, 1) if amount else strip
            old = packed[side][group]
            packed[side][group] = moved if old is None else jnp.where(hit, moved, old)
    for group in range(2):
        up[group * rows : (group + 1) * rows] = packed[0][group]
        down[group * rows : (group + 1) * rows] = packed[1][group]


def forward(
    e, h, k, layer, monitor, before, after, own, left, right,
    out, planes, kext, kstrip, lext, lstrip, fe, fh, *, cx
):
    rows = cx + 8
    gx, gy = lax.axis_index("gx"), lax.axis_index("gy")
    first_x, last_x = gx == 0, gx == lax.axis_size("gx") - 1
    first_y, last_y = gy == 0, gy == lax.axis_size("gy") - 1
    width = e.shape[1]
    for dst, src, count in ((fe, e, 3 * NZ), (fh, h, 3 * NZ), (kext, k, NZ)):
        for p in range(count):
            dst[p * rows : p * rows + cx] = src[p * cx : (p + 1) * cx]

    def put(dst, plane, count, row, value, outside):
        dst[pl.ds(plane * rows + row, count, stride=rows), :] = jnp.where(outside, 0.0, value)

    put(fe, 0, 3 * NZ, cx, after[0 : 3 * NZ], last_x)
    put(fh, 0, 3 * NZ, cx, after[3 * NZ : 6 * NZ], last_x)
    put(kext, 0, NZ, cx, after[6 * NZ : 7 * NZ], last_x)
    put(fe, NZ, 2 * NZ, cx + 1, after[7 * NZ : 9 * NZ], last_x)
    put(fe, 0, 3 * NZ, rows - 1, before[0 : 3 * NZ], first_x)
    put(fh, 0, 3 * NZ, rows - 1, before[3 * NZ : 6 * NZ], first_x)
    put(kext, 0, NZ, rows - 1, before[6 * NZ : 7 * NZ], first_x)
    put(fe, 0, 3 * NZ, rows - 2, before[7 * NZ : 10 * NZ], first_x)
    put(fh, NZ, 2 * NZ, rows - 2, before[10 * NZ : 12 * NZ], first_x)
    lext[0:cx] = layer[...].astype(F32)
    lext[cx:rows] = after[9 * NZ + 16 : 9 * NZ + 24]
    lext[rows - 1 : rows] = before[12 * NZ + 16 : 12 * NZ + 17]

    lane = iota((rows, LANES), 1)
    column = lane % GROUP
    strips = []
    for field in range(8):
        group, slot = divmod(field, 4)
        mine = own[field * rows : (field + 1) * rows]
        low = jnp.where(first_y, 0.0, left[group * rows : (group + 1) * rows])
        high = jnp.where(last_y, 0.0, right[group * rows : (group + 1) * rows])
        low = pltpu.roll(low, (-2 * slot) % LANES, 1) if slot else low
        high = pltpu.roll(high, (6 - 2 * slot) % LANES, 1) if slot != 3 else high
        value = jnp.where(column < 4, mine, pltpu.roll(mine, 4, 1))
        value = jnp.where(column < 2, low, jnp.where(column >= 6, high, value))
        strips.append(value)
    kstrip[...] = strips[6]
    lstrip[...] = strips[7]
    es, hs, ks = strips[0:3], strips[3:6], HALF * strips[6]

    row = iota((rows, width), 0)
    inside = jnp.logical_not(first_x & (row >= rows - 2))
    row = iota((rows, LANES), 0)
    inside_strip = jnp.logical_not((first_x & (row >= rows - 2)) | (first_y & (column < 2)))
    wide_lane = iota((rows, width), 1)
    shown = monitor[...]

    def next_x(v):
        return pltpu.roll(v, rows - 1, 0)

    def prev_x(v):
        return pltpu.roll(v, 1, 0)

    def strip_to(strip, source, target):
        moved = pltpu.roll(strip, (target - source) % LANES, 1)
        if width == LANES:
            return moved
        return jnp.concatenate([moved] * (width // LANES), axis=1)

    def next_y(v, strip, z):
        edge = strip_to(strip, GROUP * z + 6, (width - 1) % LANES)
        return jnp.where(wide_lane == width - 1, edge, pltpu.roll(v, width - 1, 1))

    def prev_y(v, strip, z):
        edge = strip_to(strip, GROUP * z + 1, 0)
        return jnp.where(wide_lane == 0, edge, pltpu.roll(v, 1, 1))

    def strip_next_y(v):
        return pltpu.roll(v, LANES - 1, 1)

    def strip_prev_y(v):
        return pltpu.roll(v, 1, 1)

    def strip_next_z(v):
        return jnp.where(lane >= LANES - GROUP, 0.0, pltpu.roll(v, LANES - GROUP, 1))

    def strip_prev_z(v):
        return jnp.where(lane < GROUP, 0.0, pltpu.roll(v, GROUP, 1))

    def load(ref, comp, z):
        p = comp * NZ + z
        return ref[p * rows : (p + 1) * rows]

    for moment in range(2):
        ex, ey, ez = es
        hx, hy, hz = hs
        hx = hx - HALF * ((strip_next_y(ez) - ez) - (strip_next_z(ey) - ey))
        hy = hy - HALF * ((strip_next_z(ex) - ex) - (next_x(ez) - ez))
        hz = hz - HALF * ((next_x(ey) - ey) - (strip_next_y(ex) - ex))
        new_h = [jnp.where(inside_strip, v, 0.0) for v in (hx, hy, hz)]
        hx, hy, hz = new_h
        new_e = [
            ex + ks * ((hz - strip_prev_y(hz)) - (hy - strip_prev_z(hy))),
            ey + ks * ((hx - strip_prev_z(hx)) - (hz - prev_x(hz))),
            ez + ks * ((hy - prev_x(hy)) - (hx - strip_prev_y(hx))),
        ]
        seen_x = jnp.zeros((cx, width), F32)
        seen_y = jnp.zeros((cx, width), F32)
        zero = jnp.zeros((rows, width), F32)
        under_x, under_y = zero, zero
        ex, ey, ez = (load(fe, c, 0) for c in range(3))
        for z in range(NZ):
            above = [load(fe, c, z + 1) for c in range(3)] if z + 1 < NZ else [zero] * 3
            hx, hy, hz = (load(fh, c, z) for c in range(3))
            hx = hx - HALF * ((next_y(ez, es[2], z) - ez) - (above[1] - ey))
            hy = hy - HALF * ((above[0] - ex) - (next_x(ez) - ez))
            hz = hz - HALF * ((next_x(ey) - ey) - (next_y(ex, es[0], z) - ex))
            hx, hy, hz = (jnp.where(inside, v, 0.0) for v in (hx, hy, hz))
            kz = HALF * kext[z * rows : (z + 1) * rows]
            ex = ex + kz * ((hz - prev_y(hz, new_h[2], z)) - (hy - under_y))
            ey = ey + kz * ((hx - under_x) - (hz - prev_x(hz)))
            ez = ez + kz * ((hy - prev_x(hy)) - (hx - prev_y(hx, new_h[0], z)))
            hit = shown == z
            seen_x = jnp.where(hit, ex[:cx], seen_x)
            seen_y = jnp.where(hit, ey[:cx], seen_y)
            for c, (ev, hv) in enumerate(((ex, hx), (ey, hy), (ez, hz))):
                p = c * NZ + z
                if moment == 0:
                    fe[p * rows : (p + 1) * rows] = ev
                    fh[p * rows : (p + 1) * rows] = hv
                else:
                    out[p * cx : (p + 1) * cx] = ev[:cx]
            under_x, under_y = hx, hy
            ex, ey, ez = above
        planes[2 * moment * cx : (2 * moment + 1) * cx] = seen_x
        planes[(2 * moment + 1) * cx : (2 * moment + 2) * cx] = seen_y
        es, hs = new_e, new_h


def tables(far_table, source_table, *, cy, dirs, count):
    gy = lax.axis_index("gy")
    length = cy * count
    wide = 2 * dirs
    for s in range(count):
        sender = (gy - s + count) % count
        for f, factor in enumerate(FACTORS):
            y = sender * cy + iota((cy, wide), 0)
            lane = iota((cy, wide), 1)
            b = gy * dirs + lane % dirs
            turn = (b - DIRS // 2) * factor * y - jnp.where(lane >= dirs, length, 0)
            far_table[s * cy : (s + 1) * cy, f * wide : (f + 1) * wide] = cos_turn(turn, length)
            line = iota((wide, cy + LANES), 0)
            lane = iota((wide, cy + LANES), 1)
            near = lane % GROUP
            near = jnp.where(near < 4, near - 2, near + cy - 6)
            y = gy * cy + jnp.where(lane < cy, lane, near)
            b = sender * dirs + line % dirs
            turn = (b - DIRS // 2) * factor * y + jnp.where(line >= dirs, length, 0)
            base = (s * 2 + f) * wide
            source_table[base : base + wide] = cos_turn(turn, length) * (1.0 / DIRS)


def project_y(*refs, cx, cy, dirs, count):
    blocks, table, out = refs[:count], refs[count], refs[count + 1]
    total = None
    for s in range(count):
        part = dot(blocks[s][...], table[s * cy : (s + 1) * cy])
        total = part if total is None else total + part
    wide = 2 * dirs
    sign = jnp.where(iota((2 * cx, wide), 1) < dirs, 1.0, -1.0)
    for f, omega in enumerate(OMEGAS):
        value = None
        for moment in range(2):
            tick = omega * (moment + 1)
            part = total[2 * cx * moment : 2 * cx * (moment + 1), f * wide : (f + 1) * wide]
            part = math.cos(tick) * (part * sign) - math.sin(tick) * swap(part, dirs)
            value = part if value is None else value + part
        out[f * 2 * cx : (f + 1) * 2 * cx] = value


def project_x(*refs, cx, dirs_x, dirs_y, count, scale):
    blocks, out = refs[:count], refs[count]
    gx = lax.axis_index("gx")
    length = cx * count
    wide = 2 * dirs_y
    lane = iota((dirs_x, 2 * length), 1)
    a = gx * dirs_x + iota((dirs_x, 2 * length), 0)
    slot = lane % length
    x = (gx - slot // cx + count) % count * cx + slot % cx
    sign = jnp.where(iota((length, wide), 1) < dirs_y, 1.0, -1.0)
    for f, factor in enumerate(FACTORS):
        turn = (a - DIRS // 2) * factor * x - jnp.where(lane >= length, length, 0)
        table = cos_turn(turn, length) * scale
        for c in range(2):
            base = (2 * f + c) * cx
            value = jnp.concatenate([ref[base : base + cx] for ref in blocks], axis=0)
            value = jnp.concatenate([value, swap(value, dirs_y) * sign], axis=0)
            field = dot(table, value)
            out[f, c, 0] = field[:, :dirs_y]
            out[f, c, 1] = field[:, dirs_y:]


def spread_x(residual, *outs, cx, dirs_x, dirs_y, count):
    gx = lax.axis_index("gx")
    length = cx * count
    rows = cx + 8
    lane = iota((count * rows, 2 * dirs_x), 1)
    line = iota((count * rows, 2 * dirs_x), 0)
    slot = line % rows
    slot = jnp.where(slot >= cx + 4, slot - rows, slot)
    x = (gx + line // rows) % count * cx + slot
    a = gx * dirs_x + lane % dirs_x
    for f, factor in enumerate(FACTORS):
        turn = (a - DIRS // 2) * factor * x - jnp.where(lane >= dirs_x, length, 0)
        table = cos_turn(turn, length)
        for c in range(2):
            real, imag = residual[f, c, 0], residual[f, c, 1]
            value = jnp.concatenate(
                [jnp.concatenate([real, imag], axis=1), jnp.concatenate([-imag, real], axis=1)], axis=0
            )
            part = dot(table, value)
            pair = 2 * f + c
            for s in range(count):
                base = s * rows
                outs[s][pair * cx : (pair + 1) * cx] = part[base : base + cx]
                edge = 4 * cx + 2 * pair
                outs[s][edge : edge + 1] = part[base + cx : base + cx + 1]
                outs[s][edge + 1 : edge + 2] = part[base + rows - 1 : base + rows]


def adjoint(*refs, cx, cy, dirs, count):
    blocks = refs[:count]
    table, kext, kstrip, lext, lstrip, out = refs[count : count + 6]
    rows = cx + 8
    wide = 2 * dirs
    first_x, first_y = lax.axis_index("gx") == 0, lax.axis_index("gy") == 0
    sign = jnp.where(iota((rows, wide), 1) < dirs, -1.0, 1.0)
    drive = None
    for s in range(count):
        for f, omega in enumerate(OMEGAS):
            parts = [[], []]
            for c in range(2):
                pair = 2 * f + c
                edge = 4 * cx + 2 * pair
                value = jnp.concatenate(
                    [
                        blocks[s][pair * cx : (pair + 1) * cx],
                        blocks[s][edge : edge + 1],
                        jnp.zeros((6, wide), F32),
                        blocks[s][edge + 1 : edge + 2],
                    ],
                    axis=0,
                )
                turned = swap(value, dirs) * sign
                for moment in range(2):
                    tick = omega * (moment + 1)
                    parts[moment].append(math.cos(tick) * value + math.sin(tick) * turned)
            left = jnp.concatenate(parts[0] + parts[1], axis=0)
            base = (s * 2 + f) * wide
            part = dot(left, table[base : base + wide])
            drive = part if drive is None else drive + part
    first = [-HALF * drive[c * rows : (c + 1) * rows] for c in range(2)]
    second = [drive[(2 + c) * rows : (2 + c) * rows + cx, :cy] for c in range(2)]
    ax, ay = (v[:, :cy] for v in first)
    sx, sy = (v[:, cy:] for v in first)
    row = iota((rows, cy), 0)
    inside = jnp.logical_not(first_x & (row >= rows - 2))
    lane = iota((rows, LANES), 1)
    row = iota((rows, LANES), 0)
    inside_strip = jnp.logical_not((first_x & (row >= rows - 2)) | (first_y & (lane % GROUP < 2)))
    wide_lane = iota((rows, cy), 1)
    layer = lext[...]

    hit = lstrip[...] == (lane // GROUP).astype(F32)
    ks = kstrip[...]
    sx = jnp.where(hit, sx * ks, 0.0)
    sy = jnp.where(hit, sy * ks, 0.0)

    def next_z(v):
        return jnp.where(lane >= LANES - GROUP, 0.0, pltpu.roll(v, LANES - GROUP, 1))

    def next_x(v):
        return pltpu.roll(v, rows - 1, 0)

    def prev_x(v):
        return pltpu.roll(v, 1, 0)

    def strip_to(strip, source, target):
        moved = pltpu.roll(strip, (target - source) % LANES, 1)
        if cy == LANES:
            return moved
        return jnp.concatenate([moved] * (cy // LANES), axis=1)

    hsx = jnp.where(inside_strip, HALF * (next_z(sy) - sy), 0.0)
    hsz = -HALF * ((next_x(sy) - sy) - (pltpu.roll(sx, LANES - 1, 1) - sx))
    hsz = jnp.where(inside_strip, hsz, 0.0)
    zero = jnp.zeros((rows, cy), F32)
    under_x, under_y = zero, zero

    def source(z):
        kz = kext[z * rows : (z + 1) * rows]
        hit = layer == float(z)
        return jnp.where(hit, ax * kz, 0.0), jnp.where(hit, ay * kz, 0.0)

    def prev_y(v, strip, z):
        edge = strip_to(strip, GROUP * z + 1, 0)
        return jnp.where(wide_lane == 0, edge, pltpu.roll(v, 1, 1))

    ex, ey = source(0)
    for z in range(NZ):
        above_x, above_y = source(z + 1) if z + 1 < NZ else (zero, zero)
        hx = HALF * (above_y - ey)
        hy = -HALF * (above_x - ex)
        edge = strip_to(sx, GROUP * z + 6, (cy - 1) % LANES)
        right = jnp.where(wide_lane == cy - 1, edge, pltpu.roll(ex, cy - 1, 1))
        hz = -HALF * ((next_x(ey) - ey) - (right - ex))
        hx, hy, hz = (jnp.where(inside, v, 0.0) for v in (hx, hy, hz))
        kz = HALF * kext[z * rows : z * rows + cx]
        hit = layer[:cx] == float(z)
        jx = jnp.where(hit, second[0], 0.0)
        jy = jnp.where(hit, second[1], 0.0)
        curl_x = (hz - prev_y(hz, hsz, z)) - (hy - under_y)
        curl_y = (hx - under_x) - (hz - prev_x(hz))
        curl_z = (hy - prev_x(hy)) - (hx - prev_y(hx, hsx, z))
        out[z * cx : (z + 1) * cx] = ex[:cx] + kz * (curl_x[:cx] - jx)
        out[(NZ + z) * cx : (NZ + z + 1) * cx] = ey[:cx] + kz * (curl_y[:cx] - jy)
        out[(2 * NZ + z) * cx : (2 * NZ + z + 1) * cx] = kz * curl_z[:cx]
        under_x, under_y = hx, hy
        ex, ey = above_x, above_y


def shift(value, axis, steps):
    count = lax.axis_size(axis)
    return lax.ppermute(value, axis, [(i, (i + steps) % count) for i in range(count)])


def gather(value, axis):
    return [value] + [shift(value, axis, s) for s in range(1, lax.axis_size(axis))]


def per_device(e_field, h_field, inverse_permittivity, monitor_layer, source_layer, residual_far):
    cx, cy = e_field.shape[2:]
    rows = cx + 8
    nx, ny = lax.axis_size("gx"), lax.axis_size("gy")
    dirs_x, dirs_y = residual_far.shape[3:]
    part = functools.partial
    e = e_field.reshape(3 * NZ * cx, cy)
    h = h_field.reshape(3 * NZ * cx, cy)
    k = inverse_permittivity.reshape(NZ * cx, cy)

    up, down, own = call(
        part(pack_edges, cx=cx), "pack_edges",
        [(12 * NZ + 24, cy), (9 * NZ + 24, cy), (8 * cx, LANES)], far=(0, 1, 2, 3),
    )(e, h, k, source_layer)
    before = shift(up, "gx", 1)
    after = shift(down, "gx", -1)

    pieces = call(
        part(spread_x, cx=cx, dirs_x=dirs_x, dirs_y=dirs_y, count=nx), "spread_x",
        [(4 * cx + 8, 2 * dirs_y)] * nx, far=(0,),
    )(residual_far)
    far_table, source_table = call(
        part(tables, cy=cy, dirs=dirs_y, count=ny), "tables",
        [(ny * cy, 4 * dirs_y), (ny * 4 * dirs_y, cy + LANES)],
    )()

    up, down, ext = call(
        part(pack_strips, cx=cx), "pack_strips",
        [(2 * rows, LANES), (2 * rows, LANES), (8 * rows, LANES)],
    )(own, before, after)
    left = shift(up, "gy", 1)
    right = shift(down, "gy", -1)

    mixed = pieces[0]
    for s in range(1, nx):
        mixed = mixed + shift(pieces[s], "gx", s)

    e_forward, planes, kext, kstrip, lext, lstrip = call(
        part(forward, cx=cx), "forward",
        [(3 * NZ * cx, cy), (4 * cx, cy), (NZ * rows, cy), (rows, LANES), (rows, cy), (rows, LANES)],
        [pltpu.VMEM((3 * NZ * rows, cy), F32), pltpu.VMEM((3 * NZ * rows, cy), F32)],
        far=(0, 1, 2, 3, 4), far_out=(0,),
    )(e, h, k, source_layer, monitor_layer, before, after, ext, left, right)

    spectrum = call(
        part(project_y, cx=cx, cy=cy, dirs=dirs_y, count=ny), "project_y", (4 * cx, 2 * dirs_y)
    )(*gather(planes, "gy"), far_table)
    scale = 1.0 / math.sqrt(cx * nx * cy * ny)
    far_field = call(
        part(project_x, cx=cx, dirs_x=dirs_x, dirs_y=dirs_y, count=nx, scale=scale), "project_x",
        residual_far.shape, far_out=(0,),
    )(*gather(spectrum, "gx"))

    e_adjoint = call(
        part(adjoint, cx=cx, cy=cy, dirs=dirs_y, count=ny), "adjoint", (3 * NZ * cx, cy), far_out=(0,)
    )(*gather(mixed, "gy"), source_table, kext, kstrip, lext, lstrip)
    return (e_forward.reshape(e_field.shape), far_field, e_adjoint.reshape(e_field.shape))


def solution(mesh):
    in_specs = (
        P("design", None, "gx", "gy"),
        P("design", None, "gx", "gy"),
        P("design", "gx", "gy"),
        P(("design", "gx"), "gy"),
        P(("design", "gx"), "gy"),
        P("design", None, None, "gx", "gy"),
    )
    out_specs = (
        P("design", None, "gx", "gy"),
        P("design", None, None, "gx", "gy"),
        P("design", None, "gx", "gy"),
    )
    return jax.shard_map(
        per_device, mesh=mesh, in_specs=in_specs, out_specs=out_specs, check_vma=False
    )
```
